32 devices in a mesh: grp: 2 (over x), samp: 16 (over z, y, core).
Axes of the slice: x: 2, y: 2, z: 4, core: 2. Of those that a mesh axis runs over, the one named last changes fastest.
Arguments:
- genotypes: int32 [32768, 2048], P(('grp', 'samp')), parts along dimension 0, may hold values from 0 to 2
- probe_signs: int32 [32, 32768], P(None, ('grp', 'samp')), parts along dimension 1, may hold values from 0 to 1
- phenotype: float32 [32768], P(('grp', 'samp')), parts along dimension 0, may hold values from -6 to 6
- marker_mean: float32 [2048], replicated, may hold values from 0.2 to 1.8
- marker_scale: float32 [2048], replicated, may hold values from 0.5 to 4
- marker_bin: int32 [2048], replicated, may hold values from 0 to 15, as said below
Outputs:
- products: float32 [16, 33, 32768], P(None, None, ('grp', 'samp')), parts along dimension 2
- gram: float32 [32, 16, 33], P('grp'), parts along dimension 0
The draws below stay inside these ranges and needn't reach their ends.
There are 2 independent parts, one for each index of `grp`. The reference program is written for one: setup_inputs(seed, part) draws one part's arguments, and reference() takes and returns one part's arrays. A program takes and returns all parts, laid end to end along the dimension named above; an argument that names none is the same for every part. Nothing has to cross between parts.
Inputs may be any that keep to these rules, and one draw needn't show every extreme that they name: `marker_bin`: every bin holds exactly 128 markers.
All inputs are finite; a program needn't handle non-finite values.
Results may differ from the reference program's by a relative error of at most 0.0001.
Values sent between devices are 32-bit elements; how exact they have to be, the bound alone decides.
A program may use at most 128 MiB of HBM per device.

```python
import math
import jax
import jax.numpy as jnp
from jax import lax

BINS = 16
M_BIN = 128
PROBES = 32
MARKERS = 2048
VECS = 33
NSAMP = 16384


def draw_marker_bin(key, part):
    return (jax.random.permutation(key, MARKERS) // M_BIN).astype(jnp.int32)


def plant(entries, own_key, least, largest):
    index_at = [jax.random.randint(jax.random.fold_in(own_key, axis), (), 0, length) for axis, length in enumerate(entries.shape)]
    longest = entries.shape.index(max(entries.shape))
    next_to = index_at[:longest] + [(index_at[longest] + 1) % entries.shape[longest]] + index_at[longest + 1:]
    return entries.at[tuple(index_at)].set(least).at[tuple(next_to)].set(largest)


def block_levels(rng, dims, shards, low, top_value):
    def one(dim, blocks):
        steps = jax.random.uniform(jax.random.fold_in(jax.random.fold_in(rng, 6), dim), (blocks,), jnp.float32, low / len(shards), top_value / len(shards))
        return jnp.repeat(jnp.exp(steps), dims[dim] // blocks).reshape((-1,) + (1,) * (len(dims) - dim - 1))

    loudness = one(*shards[0])
    for cut in shards[1:]:
        loudness = loudness * one(*cut)
    return loudness


def scatter_about(key, dims, spread, limit, shards=(), kind=jnp.bfloat16):
    level = block_levels(key, dims, shards, -0.22, 0.18) if shards else 1.0
    entries = jax.random.normal(key, dims, jnp.float32) * spread * level
    return jnp.minimum(jnp.maximum(entries, -limit), limit).astype(kind)


def setup_inputs(seed: int = 0, part: int = 0) -> dict:
    key_of = jax.random.split(jax.random.key(seed), 7)
    part_keys = jax.random.split(jax.random.fold_in(key_of[6], part), 7)
    return {
        "genotypes": plant(jax.random.randint(part_keys[0], (NSAMP, MARKERS), 0, 3), jax.random.fold_in(part_keys[0], 1), 0, 2).astype(jnp.int32),
        "probe_signs": plant(jax.random.randint(part_keys[1], (PROBES, NSAMP), 0, 2), jax.random.fold_in(part_keys[1], 1), 0, 1).astype(jnp.int32),
        "phenotype": scatter_about(part_keys[2], (NSAMP,), 1.0, 6.0, ((0, 16),), jnp.float32),
        "marker_mean": jnp.clip(jax.random.uniform(key_of[3], (MARKERS,), jnp.float32, 0.2, 1.8), 0.2, 1.8),
        "marker_scale": jnp.clip(jnp.exp(jax.random.uniform(key_of[4], (MARKERS,), jnp.float32, math.log(0.5), math.log(4.0))), 0.5, 4.0),
        "marker_bin": draw_marker_bin(jax.random.fold_in(key_of[6], 71), part),
    }


def reference(genotypes, probe_signs, phenotype, marker_mean, marker_scale, marker_bin):
    order = jnp.argsort(marker_bin, stable=True).astype(jnp.int32)
    picked = jnp.take(genotypes, order, axis=1).astype(jnp.float32)
    standard = (picked - marker_mean[order]) * marker_scale[order]
    vectors = jnp.concatenate([(2 * probe_signs - 1).astype(jnp.float32), phenotype[None, :].astype(jnp.float32)], axis=0)
    scores = jnp.dot(standard.T, vectors.T, precision=lax.Precision.HIGHEST, preferred_element_type=jnp.float32)
    scores = scores / jnp.sqrt(jnp.float32(NSAMP))
    blocks = standard.reshape(NSAMP, BINS, M_BIN)
    weights = scores.reshape(BINS, M_BIN, VECS)
    products = jnp.einsum('skm,kmr->krs', blocks, weights, precision=lax.Precision.HIGHEST) / jnp.sqrt(jnp.float32(M_BIN))
    gram = jnp.einsum('krs,lrs->klr', products, products, precision=lax.Precision.HIGHEST) / jnp.float32(NSAMP)
    return (products, gram)
```

```python
import functools
import math

import jax
import jax.numpy as jnp
from jax import lax
from jax.experimental import pallas as pl
from jax.experimental.pallas import tpu as pltpu
from jax.sharding import PartitionSpec as P

BINS = 16
M_BIN = 128
LANES = 128
GROUP = 256
BF = jnp.bfloat16
F32 = jnp.float32
MESH = pl.DeviceIdType.MESH
NT = (((1,), (1,)), ((), ()))


def dot(a, b):
    return jnp.dot(a, b, preferred_element_type=F32)


def dot_nt(a, b):
    return lax.dot_general(a, b, NT, preferred_element_type=F32)


def high(x):
    return x.astype(BF)


def rest(x):
    return (x - x.astype(BF).astype(F32)).astype(BF)


def kernel(n, split, rows, per, total, g_hbm, probe, pheno, mean, scale, bins, out_hbm, gram,
           gbuf, gb, vec, tsend, sibrecv, rsend, rsrecv, ag, wsp, prods, gsend, grecv, gsum,
           in_sem, out_sem, sib_s, sib_r, rs_s, rs_r, ag_s, ag_r, fwd_s, gr_s, gr_r, ga_s, ga_r):
    me = lax.axis_index("samp")
    chip, core = me // 2, me % 2
    chips = n // 2
    sib = me + 1 - 2 * core
    samples, markers = g_hbm.shape
    probes = probe.shape[0]
    vecs = probes + 1
    groups = markers // GROUP
    home = chip // split

    barrier = pltpu.get_barrier_semaphore()

    @pl.loop(1, n)
    def _(s):
        pl.semaphore_signal(barrier, inc=1, device_id={"samp": lax.rem(me + s, n)}, device_id_type=MESH)

    def cg_of(q):
        return lax.rem(home + 1 + q, groups)

    def cols(q):
        return pl.ds(pl.multiple_of(cg_of(q) * GROUP, GROUP), GROUP)

    def load(q):
        return pltpu.make_async_copy(g_hbm.at[:, cols(q)], gbuf.at[q], in_sem.at[q])

    for q in range(groups):
        load(q).start()

    def to_sib(m):
        return pltpu.make_async_remote_copy(
            tsend.at[m, 1 - core], sibrecv.at[m], sib_s.at[m], sib_r.at[m],
            device_id={"samp": sib}, device_id_type=MESH)

    def to_owner(m):
        return pltpu.make_async_remote_copy(
            rsend.at[m], rsrecv.at[chip], rs_s.at[m], rs_r.at[chip],
            device_id={"samp": 2 * m + core}, device_id_type=MESH)

    def from_owner(m):
        return pltpu.make_async_remote_copy(
            rsend.at[m], rsrecv.at[m], rs_s.at[m], rs_r.at[m],
            device_id={"samp": 2 * m + core}, device_id_type=MESH)

    signs = (2 * probe[...] - 1).astype(F32)
    ph = pheno[...]
    ph_mid = ph - high(ph).astype(F32)
    vec[0:probes, :] = high(signs)
    tail = jnp.concatenate(
        [ph, ph_mid, ph_mid - high(ph_mid).astype(F32), jnp.zeros((13, samples), F32)], axis=0)
    vec[probes:probes + 16, :] = high(tail)
    sum_p = jnp.sum(signs, axis=1, keepdims=True)
    sum_y = jnp.sum(ph, axis=1, keepdims=True)

    def combine(q):
        for i in range(split):
            m = cg_of(q) * split + i
            to_sib(m).wait_recv()
            both = tsend[m, core] + sibrecv[m]
            if split == 1:
                if q == groups - 1:
                    rsrecv[m] = both
                else:
                    rsend[m] = both
                    to_owner(m).start()
            else:
                @pl.when(m == chip)
                def _():
                    rsrecv[m] = both

                @pl.when(m != chip)
                def _():
                    rsend[m] = both
                    to_owner(m).start()

    for q in range(groups):
        load(q).wait()
        part = gbuf[q].astype(F32).astype(BF)
        gb[:, cols(q)] = part
        t = dot(vec[...], part)
        mu = mean[:, cols(q)]
        tp = t[0:probes] - sum_p * mu
        ty = t[probes:probes + 1] + t[probes + 1:probes + 2] + t[probes + 2:probes + 3] - sum_y * mu
        cg = cg_of(q)
        if split == 1:
            for h in range(2):
                at = slice(h * LANES, (h + 1) * LANES)
                tsend[cg, h, 0:probes, :] = tp[:, at]
                tsend[cg, h, probes:vecs, :] = ty[:, at]
        else:
            whole = jnp.concatenate([tp, ty, jnp.zeros((split * rows - vecs, GROUP), F32)], axis=0)
            for h in range(2):
                for s in range(split):
                    tsend[cg * split + (h * split + s) // 2, s % 2] = whole[
                        s * rows:(s + 1) * rows, h * LANES:(h + 1) * LANES]
        if q == 0:
            pl.semaphore_wait(barrier, n - 1)
        for i in range(split):
            to_sib(cg * split + i).start()
        if q > 0:
            combine(q - 1)
    combine(groups - 1)

    def others(body):
        @pl.loop(1, chips)
        def _(s):
            body(lax.rem(chip + s, chips))

    others(lambda m: from_owner(m).wait_recv())
    ag[me] = jnp.sum(rsrecv[...], axis=0)

    def ag_chip(m):
        return pltpu.make_async_remote_copy(
            ag.at[me], ag.at[me], ag_s.at[m], ag_r.at[me],
            device_id={"samp": 2 * m + core}, device_id_type=MESH)

    def ag_fwd(m):
        return pltpu.make_async_remote_copy(
            ag.at[2 * m + core], ag.at[2 * m + core], fwd_s.at[m], ag_r.at[2 * m + core],
            device_id={"samp": sib}, device_id_type=MESH)

    def ag_got(d):
        return pltpu.make_async_remote_copy(
            ag.at[d], ag.at[d], fwd_s.at[chip], ag_r.at[d],
            device_id={"samp": sib}, device_id_type=MESH)

    others(lambda m: ag_chip(m).start())
    ag_fwd(chip).start()

    def pass_on(m):
        ag_got(2 * m + core).wait_recv()
        ag_fwd(m).start()

    others(pass_on)

    @pl.loop(0, chips)
    def _(s):
        ag_got(2 * lax.rem(chip + s, chips) + 1 - core).wait_recv()

    factor = 1.0 / (math.sqrt(total) * math.sqrt(M_BIN))
    if split == 1:
        got = jnp.concatenate([ag[d] for d in range(n)], axis=1)
    else:
        got = jnp.concatenate(
            [jnp.concatenate([ag[lane * split + s] for s in range(split)], axis=0)[0:vecs]
             for lane in range(n // split)], axis=1)
    sc = scale[...]
    w = got * (sc * sc * factor)
    wh, wl = high(w).astype(F32), rest(w).astype(F32)
    wm = (wh + wl) * mean[...]
    member = lax.broadcasted_iota(jnp.int32, (BINS, markers), 0) == bins[...]
    offs = []
    for r in range(vecs):
        at = slice(r * BINS, (r + 1) * BINS)
        wsp[0, at, :] = high(jnp.where(member, wh[r:r + 1], 0.0))
        wsp[1, at, :] = high(jnp.where(member, wl[r:r + 1], 0.0))
        offs.append(jnp.sum(jnp.where(member, wm[r:r + 1], 0.0), axis=1, keepdims=True))
    off = jnp.concatenate(offs, axis=0)
    half = (probes // 2) * BINS
    cuts = [(0, half), (half, 2 * half), (2 * half, vecs * BINS)]
    accs = [jnp.zeros((b - a, b - a), F32) for a, b in cuts]
    for nb in range(samples // GROUP):
        at = slice(nb * GROUP, (nb + 1) * GROUP)
        gpart = gb[at, :]
        res = dot_nt(wsp[0], gpart) + dot_nt(wsp[1], gpart) - off
        prods[:, :, at] = res.reshape(vecs, BINS, GROUP)
        hi, lo = high(res), rest(res)
        for i, (a, b) in enumerate(cuts):
            h, l = hi[a:b], lo[a:b]
            accs[i] = accs[i] + dot_nt(h, h) + dot_nt(h, l) + dot_nt(l, h)

    def out_copy(r):
        return pltpu.make_async_copy(prods.at[r], out_hbm.at[:, r, :], out_sem.at[r])

    @pl.loop(0, vecs)
    def _(r):
        out_copy(r).start()

    strips = []
    for acc in accs:
        size = acc.shape[0]
        same = (lax.broadcasted_iota(jnp.int32, (size, size), 0) // BINS
                == lax.broadcasted_iota(jnp.int32, (size, size), 1) // BINS)
        strips.append(jnp.sum(jnp.where(same, acc, 0.0).reshape(size // BINS, BINS, size), axis=0))
    strips.append(jnp.zeros((BINS, LANES - BINS), F32))
    flat = jnp.concatenate(strips, axis=1)
    width = flat.shape[1] // LANES
    for k in range(BINS):
        for t in range(width):
            p = k * width + t
            gsend[p // per, p % per:p % per + 1, :] = flat[k:k + 1, t * LANES:(t + 1) * LANES]
    for p in range(BINS * width, n * per):
        gsend[p // per, p % per:p % per + 1, :] = jnp.zeros((1, LANES), F32)

    def gr(d, slot):
        return pltpu.make_async_remote_copy(
            gsend.at[d], grecv.at[slot], gr_s.at[d], gr_r.at[slot],
            device_id={"samp": d}, device_id_type=MESH)

    def ga(d, slot):
        return pltpu.make_async_remote_copy(
            gsum.at[slot], gsum.at[slot], ga_s.at[d], ga_r.at[slot],
            device_id={"samp": d}, device_id_type=MESH)

    def peers(body):
        @pl.loop(1, n)
        def _(s):
            body(lax.rem(me + s, n))

    peers(lambda d: gr(d, me).start())
    grecv[me] = gsend[me]
    peers(lambda d: gr(d, d).wait_recv())
    gsum[me] = jnp.sum(grecv[...], axis=0) * (1.0 / total)
    peers(lambda d: ga(d, me).start())
    peers(lambda d: ga(d, d).wait_recv())
    gram[...] = gsum[...]

    def finish(d):
        gr(d, me).wait_send()
        ga(d, me).wait_send()

    peers(finish)

    def finish_chip(m):
        to_owner(m).wait_send()
        ag_chip(m).wait_send()

    others(finish_chip)

    @pl.loop(0, chips)
    def _(m):
        to_sib(m).wait_send()
        ag_fwd(m).wait_send()

    @pl.loop(0, vecs)
    def _(r):
        out_copy(r).wait()


def shards(genotypes, probe_signs, phenotype, marker_mean, marker_scale, marker_bin):
    samples, markers = genotypes.shape
    probes = probe_signs.shape[0]
    vecs = probes + 1
    n = lax.axis_size("samp")
    total = float(samples * n)
    chunks = markers // LANES
    split = n // chunks
    rows = -(-vecs // split)
    width = -(-(vecs * BINS) // LANES)
    per = -(-(BINS * width) // n)
    chips = n // 2
    groups = markers // GROUP
    vm = pltpu.VMEM
    dma = pltpu.SemaphoreType.DMA
    vspec = pl.BlockSpec(memory_space=pltpu.VMEM)
    anyspec = pl.BlockSpec(memory_space=pl.ANY)
    products, gram = pl.pallas_call(
        functools.partial(kernel, n, split, rows, per, total),
        out_shape=(jax.ShapeDtypeStruct((BINS, vecs, samples), F32),
                   jax.ShapeDtypeStruct((n, per, LANES), F32)),
        in_specs=[anyspec] + [vspec] * 5,
        out_specs=(anyspec, vspec),
        scratch_shapes=[
            vm((groups, samples, GROUP), jnp.int32),
            vm((samples, markers), BF),
            vm((probes + 16, samples), BF),
            vm((chips, 2, rows, LANES), F32),
            vm((chips, rows, LANES), F32),
            vm((chips, rows, LANES), F32),
            vm((chips, rows, LANES), F32),
            vm((n, rows, LANES), F32),
            vm((2, vecs * BINS, markers), BF),
            vm((vecs, BINS, samples), F32),
            vm((n, per, LANES), F32),
            vm((n, per, LANES), F32),
            vm((n, per, LANES), F32),
            dma((groups,)), dma((vecs,)),
            dma((chips,)), dma((chips,)), dma((chips,)), dma((chips,)),
            dma((chips,)), dma((n,)), dma((chips,)),
            dma((n,)), dma((n,)), dma((n,)), dma((n,)),
        ],
        compiler_params=pltpu.CompilerParams(
            collective_id=0, has_side_effects=True, vmem_limit_bytes=60 * 1024 * 1024),
    )(genotypes, probe_signs, phenotype[None, :], marker_mean[None, :],
      marker_scale[None, :], marker_bin[None, :])
    gram = gram.reshape(n * per, LANES)[:BINS * width].reshape(BINS, width * LANES)
    gram = gram[:, :vecs * BINS].reshape(BINS, vecs, BINS).transpose(0, 2, 1)
    return products, gram


def solution(mesh):
    in_specs = (
        P(("grp", "samp"), None),
        P(None, ("grp", "samp")),
        P(("grp", "samp")),
        P(),
        P(),
        P(),
    )
    out_specs = (P(None, None, ("grp", "samp")), P("grp", None, None))
    return jax.shard_map(shards, mesh=mesh, in_specs=in_specs, out_specs=out_specs, check_vma=False)
```

```python
import functools
import math

import jax
import jax.numpy as jnp
from jax import lax
from jax.experimental import pallas as pl
from jax.experimental.pallas import tpu as pltpu
from jax.sharding import PartitionSpec as P

BINS = 16
M_BIN = 128
LANES = 128
GROUP = 256
BF = jnp.bfloat16
F32 = jnp.float32
MESH = pl.DeviceIdType.MESH
NT = (((1,), (1,)), ((), ()))


def dot(a, b):
    return jnp.dot(a, b, preferred_element_type=F32)


def dot_nt(a, b):
    return lax.dot_general(a, b, NT, preferred_element_type=F32)


def high(x):
    return x.astype(BF)


def rest(x):
    return (x - x.astype(BF).astype(F32)).astype(BF)


def kernel(n, split, rows, per, total, g_hbm, probe, pheno, mean, scale, bins, out_hbm, gram,
           gbuf, gb, vec, tsend, sibrecv, rsend, rsrecv, ag, wsp, prods, offs, gsend, grecv, gsum,
           in_sem, out_sem, sib_s, sib_r, rs_s, rs_r, ag_s, ag_r, fwd_s, gr_s, gr_r, ga_s, ga_r):
    me = lax.axis_index("samp")
    chip, core = me // 2, me % 2
    chips = n // 2
    sib = me + 1 - 2 * core
    samples, markers = g_hbm.shape
    probes = probe.shape[0]
    vecs = probes + 1
    groups = markers // GROUP
    home = chip // split

    barrier = pltpu.get_barrier_semaphore()

    @pl.loop(1, n)
    def _(s):
        pl.semaphore_signal(barrier, inc=1, device_id={"samp": lax.rem(me + s, n)}, device_id_type=MESH)

    def cg_of(q):
        return lax.rem(home + 1 + q, groups)

    def cols(q):
        return pl.ds(pl.multiple_of(cg_of(q) * GROUP, GROUP), GROUP)

    def load(q):
        return pltpu.make_async_copy(g_hbm.at[:, cols(q)], gbuf.at[q], in_sem.at[q])

    for q in range(groups):
        load(q).start()

    def to_sib(m):
        return pltpu.make_async_remote_copy(
            tsend.at[m, 1 - core], sibrecv.at[m], sib_s.at[m], sib_r.at[m],
            device_id={"samp": sib}, device_id_type=MESH)

    def to_owner(m):
        return pltpu.make_async_remote_copy(
            rsend.at[m], rsrecv.at[chip], rs_s.at[m], rs_r.at[chip],
            device_id={"samp": 2 * m + core}, device_id_type=MESH)

    def from_owner(m):
        return pltpu.make_async_remote_copy(
            rsend.at[m], rsrecv.at[m], rs_s.at[m], rs_r.at[m],
            device_id={"samp": 2 * m + core}, device_id_type=MESH)

    signs = (2 * probe[...] - 1).astype(F32)
    ph = pheno[...]
    ph_mid = ph - high(ph).astype(F32)
    vec[0:probes, :] = high(signs)
    tail = jnp.concatenate(
        [ph, ph_mid, ph_mid - high(ph_mid).astype(F32), jnp.zeros((13, samples), F32)], axis=0)
    vec[probes:probes + 16, :] = high(tail)
    sum_p = jnp.sum(signs, axis=1, keepdims=True)
    sum_y = jnp.sum(ph, axis=1, keepdims=True)

    def combine(q):
        for i in range(split):
            m = cg_of(q) * split + i
            to_sib(m).wait_recv()
            both = tsend[m, core] + sibrecv[m]
            if split == 1:
                if q == groups - 1:
                    rsrecv[m] = both
                else:
                    rsend[m] = both
                    to_owner(m).start()
            else:
                @pl.when(m == chip)
                def _():
                    rsrecv[m] = both

                @pl.when(m != chip)
                def _():
                    rsend[m] = both
                    to_owner(m).start()

    for q in range(groups):
        load(q).wait()
        part = gbuf[q].astype(F32).astype(BF)
        gb[:, cols(q)] = part
        t = dot(vec[...], part)
        mu = mean[:, cols(q)]
        tp = t[0:probes] - sum_p * mu
        ty = t[probes:probes + 1] + t[probes + 1:probes + 2] + t[probes + 2:probes + 3] - sum_y * mu
        cg = cg_of(q)
        if split == 1:
            for h in range(2):
                at = slice(h * LANES, (h + 1) * LANES)
                tsend[cg, h, 0:probes, :] = tp[:, at]
                tsend[cg, h, probes:vecs, :] = ty[:, at]
        else:
            whole = jnp.concatenate([tp, ty, jnp.zeros((split * rows - vecs, GROUP), F32)], axis=0)
            for h in range(2):
                for s in range(split):
                    tsend[cg * split + (h * split + s) // 2, s % 2] = whole[
                        s * rows:(s + 1) * rows, h * LANES:(h + 1) * LANES]
        if q == 0:
            pl.semaphore_wait(barrier, n - 1)
        for i in range(split):
            to_sib(cg * split + i).start()
        if q > 0:
            combine(q - 1)
    combine(groups - 1)

    def others(body):
        @pl.loop(1, chips)
        def _(s):
            body(lax.rem(chip + s, chips))

    others(lambda m: from_owner(m).wait_recv())
    ag[me] = jnp.sum(rsrecv[...], axis=0)

    def ag_chip(m):
        return pltpu.make_async_remote_copy(
            ag.at[me], ag.at[me], ag_s.at[m], ag_r.at[me],
            device_id={"samp": 2 * m + core}, device_id_type=MESH)

    def ag_fwd(m):
        return pltpu.make_async_remote_copy(
            ag.at[2 * m + core], ag.at[2 * m + core], fwd_s.at[m], ag_r.at[2 * m + core],
            device_id={"samp": sib}, device_id_type=MESH)

    def ag_got(d):
        return pltpu.make_async_remote_copy(
            ag.at[d], ag.at[d], fwd_s.at[chip], ag_r.at[d],
            device_id={"samp": sib}, device_id_type=MESH)

    others(lambda m: ag_chip(m).start())
    ag_fwd(chip).start()

    factor = 1.0 / (math.sqrt(total) * math.sqrt(M_BIN))
    depth = vecs * BINS
    prods[...] = jnp.zeros_like(prods)
    offs[...] = jnp.zeros_like(offs)

    def receive(s):
        for i in range(split):
            m = lax.rem(home + s, groups) * split + i

            @pl.when(m != chip)
            def _():
                ag_got(2 * m + core).wait_recv()
                ag_fwd(m).start()

    def multiply(s):
        cg = lax.rem(home + s, groups)
        for i in range(split):
            ag_got(2 * (cg * split + i) + 1 - core).wait_recv()
        at = pl.ds(pl.multiple_of(cg * GROUP, GROUP), GROUP)
        lanes = []
        for h in range(2):
            first = (2 * cg + h) * split
            part = [ag[first + i] for i in range(split)]
            lanes.append(part[0] if split == 1 else jnp.concatenate(part, axis=0)[0:vecs])
        sc = scale[:, at]
        w = jnp.concatenate(lanes, axis=1) * (sc * sc * factor)
        wh, wl = high(w).astype(F32), rest(w).astype(F32)
        wm = (wh + wl) * mean[:, at]
        member = lax.broadcasted_iota(jnp.int32, (BINS, GROUP), 0) == bins[:, at]
        for r in range(vecs):
            row = slice(r * BINS, (r + 1) * BINS)
            wsp[row, :] = high(jnp.where(member, wh[r:r + 1], 0.0))
            wsp[depth + r * BINS:depth + (r + 1) * BINS, :] = high(jnp.where(member, wl[r:r + 1], 0.0))
            o = jnp.where(member, wm[r:r + 1], 0.0)
            offs[row, :] += o[:, :LANES] + o[:, LANES:]
        for nb in range(samples // GROUP):
            span = slice(nb * GROUP, (nb + 1) * GROUP)
            res = dot_nt(wsp[...], gb[span, at])
            prods[:, span] += res[:depth] + res[depth:]

    if split > 1:
        receive(0)

    @pl.loop(1, groups)
    def _(s):
        receive(s)
        multiply(s - 1)

    multiply(groups - 1)
    off = jnp.sum(offs[...], axis=1, keepdims=True)
    half = (probes // 2) * BINS
    cuts = [(0, half), (half, 2 * half), (2 * half, depth)]
    accs = [jnp.zeros((b - a, b - a), F32) for a, b in cuts]

    def out_copy(nb):
        span = slice(nb * GROUP, (nb + 1) * GROUP)
        return pltpu.make_async_copy(prods.at[:, span], out_hbm.at[:, span], out_sem.at[nb])

    for nb in range(samples // GROUP):
        span = slice(nb * GROUP, (nb + 1) * GROUP)
        res = prods[:, span] - off
        prods[:, span] = res
        out_copy(nb).start()
        hi, lo = high(res), rest(res)
        for i, (a, b) in enumerate(cuts):
            h, l = hi[a:b], lo[a:b]
            accs[i] = accs[i] + dot_nt(h, h) + dot_nt(h, l) + dot_nt(l, h)

    strips = []
    for acc in accs:
        size = acc.shape[0]
        same = (lax.broadcasted_iota(jnp.int32, (size, size), 0) // BINS
                == lax.broadcasted_iota(jnp.int32, (size, size), 1) // BINS)
        strips.append(jnp.sum(jnp.where(same, acc, 0.0).reshape(size // BINS, BINS, size), axis=0))
    strips.append(jnp.zeros((BINS, LANES - BINS), F32))
    flat = jnp.concatenate(strips, axis=1)
    width = flat.shape[1] // LANES
    for k in range(BINS):
        for t in range(width):
            p = k * width + t
            gsend[p // per, p % per:p % per + 1, :] = flat[k:k + 1, t * LANES:(t + 1) * LANES]
    for p in range(BINS * width, n * per):
        gsend[p // per, p % per:p % per + 1, :] = jnp.zeros((1, LANES), F32)

    def gr(d, slot):
        return pltpu.make_async_remote_copy(
            gsend.at[d], grecv.at[slot], gr_s.at[d], gr_r.at[slot],
            device_id={"samp": d}, device_id_type=MESH)

    def ga(d, slot):
        return pltpu.make_async_remote_copy(
            gsum.at[slot], gsum.at[slot], ga_s.at[d], ga_r.at[slot],
            device_id={"samp": d}, device_id_type=MESH)

    def peers(body):
        @pl.loop(1, n)
        def _(s):
            body(lax.rem(me + s, n))

    peers(lambda d: gr(d, me).start())
    grecv[me] = gsend[me]
    peers(lambda d: gr(d, d).wait_recv())
    gsum[me] = jnp.sum(grecv[...], axis=0) * (1.0 / total)
    peers(lambda d: ga(d, me).start())
    peers(lambda d: ga(d, d).wait_recv())
    gram[...] = gsum[...]

    def finish(d):
        gr(d, me).wait_send()
        ga(d, me).wait_send()

    peers(finish)

    def finish_chip(m):
        to_owner(m).wait_send()
        ag_chip(m).wait_send()

    others(finish_chip)

    @pl.loop(0, chips)
    def _(m):
        to_sib(m).wait_send()
        ag_fwd(m).wait_send()

    for nb in range(samples // GROUP):
        out_copy(nb).wait()


def shards(genotypes, probe_signs, phenotype, marker_mean, marker_scale, marker_bin):
    samples, markers = genotypes.shape
    probes = probe_signs.shape[0]
    vecs = probes + 1
    n = lax.axis_size("samp")
    total = float(samples * n)
    chunks = markers // LANES
    split = n // chunks
    rows = -(-vecs // split)
    width = -(-(vecs * BINS) // LANES)
    per = -(-(BINS * width) // n)
    chips = n // 2
    groups = markers // GROUP
    vm = pltpu.VMEM
    dma = pltpu.SemaphoreType.DMA
    vspec = pl.BlockSpec(memory_space=pltpu.VMEM)
    anyspec = pl.BlockSpec(memory_space=pl.ANY)
    products, gram = pl.pallas_call(
        functools.partial(kernel, n, split, rows, per, total),
        out_shape=(jax.ShapeDtypeStruct((vecs * BINS, samples), F32),
                   jax.ShapeDtypeStruct((n, per, LANES), F32)),
        in_specs=[anyspec] + [vspec] * 5,
        out_specs=(anyspec, vspec),
        scratch_shapes=[
            vm((groups, samples, GROUP), jnp.int32),
            vm((samples, markers), BF),
            vm((probes + 16, samples), BF),
            vm((chips, 2, rows, LANES), F32),
            vm((chips, rows, LANES), F32),
            vm((chips, rows, LANES), F32),
            vm((chips, rows, LANES), F32),
            vm((n, rows, LANES), F32),
            vm((2 * vecs * BINS, GROUP), BF),
            vm((vecs * BINS, samples), F32),
            vm((vecs * BINS, LANES), F32),
            vm((n, per, LANES), F32),
            vm((n, per, LANES), F32),
            vm((n, per, LANES), F32),
            dma((groups,)), dma((samples // GROUP,)),
            dma((chips,)), dma((chips,)), dma((chips,)), dma((chips,)),
            dma((chips,)), dma((n,)), dma((chips,)),
            dma((n,)), dma((n,)), dma((n,)), dma((n,)),
        ],
        compiler_params=pltpu.CompilerParams(
            collective_id=0, has_side_effects=True, vmem_limit_bytes=60 * 1024 * 1024),
    )(genotypes, probe_signs, phenotype[None, :], marker_mean[None, :],
      marker_scale[None, :], marker_bin[None, :])
    gram = gram.reshape(n * per, LANES)[:BINS * width].reshape(BINS, width * LANES)
    gram = gram[:, :vecs * BINS].reshape(BINS, vecs, BINS).transpose(0, 2, 1)
    return products.reshape(vecs, BINS, samples).transpose(1, 0, 2), gram


def solution(mesh):
    in_specs = (
        P(("grp", "samp"), None),
        P(None, ("grp", "samp")),
        P(("grp", "samp")),
        P(),
        P(),
        P(),
    )
    out_specs = (P(None, None, ("grp", "samp")), P("grp", None, None))
    return jax.shard_map(shards, mesh=mesh, in_specs=in_specs, out_specs=out_specs, check_vma=False)
```

```python
import functools
import math

import jax
import jax.numpy as jnp
from jax import lax
from jax.experimental import pallas as pl
from jax.experimental.pallas import tpu as pltpu
from jax.sharding import PartitionSpec as P

BINS = 16
M_BIN = 128
LANES = 128
GROUP = 256
BF = jnp.bfloat16
F32 = jnp.float32
MESH = pl.DeviceIdType.MESH
NT = (((1,), (1,)), ((), ()))


def dot(a, b):
    return jnp.dot(a, b, preferred_element_type=F32)


def dot_nt(a, b):
    return lax.dot_general(a, b, NT, preferred_element_type=F32)


def high(x):
    return x.astype(BF)


def rest(x):
    return (x - x.astype(BF).astype(F32)).astype(BF)


def kernel(n, split, rows, per, total, g_hbm, probe_hbm, pheno_hbm, mean_hbm, scale_hbm, bins_hbm, prods, gram,
           probe, pheno, mean, scale, bins,
           gbuf, gb, vec, tsend, sibrecv, rsend, rsrecv, ag, wsp, offs, gsend, grecv, gsum,
           small_sem, in_sem, sib_s, sib_r, rs_s, rs_r, ag_s, ag_r, fwd_s, gr_s, gr_r, ga_s, ga_r):
    me = lax.axis_index("samp")
    chip, core = me // 2, me % 2
    chips = n // 2
    sib = me + 1 - 2 * core
    samples, markers = g_hbm.shape
    probes = probe.shape[0]
    vecs = probes + 1
    groups = markers // GROUP
    home = chip // split

    barrier = pltpu.get_barrier_semaphore()

    @pl.loop(1, n)
    def _(s):
        pl.semaphore_signal(barrier, inc=1, device_id={"samp": lax.rem(me + s, n)}, device_id_type=MESH)

    def cg_of(q):
        return lax.rem(home + 1 + q, groups)

    def cols(q):
        return pl.ds(pl.multiple_of(cg_of(q) * GROUP, GROUP), GROUP)

    def load(q):
        return pltpu.make_async_copy(g_hbm.at[:, cols(q)], gbuf.at[q], in_sem.at[q])

    small = [pltpu.make_async_copy(src, dst, small_sem.at[i]) for i, (src, dst) in enumerate(
        [(probe_hbm, probe), (pheno_hbm, pheno), (mean_hbm, mean), (scale_hbm, scale), (bins_hbm, bins)])]
    for copy in small:
        copy.start()
    for q in range(groups):
        load(q).start()

    def to_sib(m):
        return pltpu.make_async_remote_copy(
            tsend.at[m, 1 - core], sibrecv.at[m], sib_s.at[m], sib_r.at[m],
            device_id={"samp": sib}, device_id_type=MESH)

    def to_owner(m):
        return pltpu.make_async_remote_copy(
            rsend.at[m], rsrecv.at[chip], rs_s.at[m], rs_r.at[chip],
            device_id={"samp": 2 * m + core}, device_id_type=MESH)

    def from_owner(m):
        return pltpu.make_async_remote_copy(
            rsend.at[m], rsrecv.at[m], rs_s.at[m], rs_r.at[m],
            device_id={"samp": 2 * m + core}, device_id_type=MESH)

    for copy in small:
        copy.wait()
    signs = (2 * probe[...] - 1).astype(F32)
    ph = pheno[...]
    ph_mid = ph - high(ph).astype(F32)
    vec[0:probes, :] = high(signs)
    tail = jnp.concatenate(
        [ph, ph_mid, ph_mid - high(ph_mid).astype(F32), jnp.zeros((13, samples), F32)], axis=0)
    vec[probes:probes + 16, :] = high(tail)
    sum_p = jnp.sum(signs, axis=1, keepdims=True)
    sum_y = jnp.sum(ph, axis=1, keepdims=True)

    def combine(q):
        for i in range(split):
            m = cg_of(q) * split + i
            to_sib(m).wait_recv()
            both = tsend[m, core] + sibrecv[m]
            if split == 1:
                if q == groups - 1:
                    rsrecv[m] = both
                else:
                    rsend[m] = both
                    to_owner(m).start()
            else:
                @pl.when(m == chip)
                def _():
                    rsrecv[m] = both

                @pl.when(m != chip)
                def _():
                    rsend[m] = both
                    to_owner(m).start()

    for q in range(groups):
        load(q).wait()
        part = gbuf[q].astype(F32).astype(BF)
        gb[:, cols(q)] = part
        t = dot(vec[...], part)
        mu = mean[:, cols(q)]
        tp = t[0:probes] - sum_p * mu
        ty = t[probes:probes + 1] + t[probes + 1:probes + 2] + t[probes + 2:probes + 3] - sum_y * mu
        cg = cg_of(q)
        if split == 1:
            for h in range(2):
                at = slice(h * LANES, (h + 1) * LANES)
                tsend[cg, h, 0:probes, :] = tp[:, at]
                tsend[cg, h, probes:vecs, :] = ty[:, at]
        else:
            whole = jnp.concatenate([tp, ty, jnp.zeros((split * rows - vecs, GROUP), F32)], axis=0)
            for h in range(2):
                for s in range(split):
                    tsend[cg * split + (h * split + s) // 2, s % 2] = whole[
                        s * rows:(s + 1) * rows, h * LANES:(h + 1) * LANES]
        if q == 0:
            pl.semaphore_wait(barrier, n - 1)
        for i in range(split):
            to_sib(cg * split + i).start()
        if q > 0:
            combine(q - 1)
    combine(groups - 1)

    def others(body):
        @pl.loop(1, chips)
        def _(s):
            body(lax.rem(chip + s, chips))

    others(lambda m: from_owner(m).wait_recv())
    ag[me] = jnp.sum(rsrecv[...], axis=0)

    def ag_chip(m):
        return pltpu.make_async_remote_copy(
            ag.at[me], ag.at[me], ag_s.at[m], ag_r.at[me],
            device_id={"samp": 2 * m + core}, device_id_type=MESH)

    def ag_fwd(m):
        return pltpu.make_async_remote_copy(
            ag.at[2 * m + core], ag.at[2 * m + core], fwd_s.at[m], ag_r.at[2 * m + core],
            device_id={"samp": sib}, device_id_type=MESH)

    def ag_got(d):
        return pltpu.make_async_remote_copy(
            ag.at[d], ag.at[d], fwd_s.at[chip], ag_r.at[d],
            device_id={"samp": sib}, device_id_type=MESH)

    others(lambda m: ag_chip(m).start())
    ag_fwd(chip).start()

    factor = 1.0 / (math.sqrt(total) * math.sqrt(M_BIN))
    depth = vecs * BINS
    prods[...] = jnp.zeros_like(prods)
    offs[...] = jnp.zeros_like(offs)

    def receive(s):
        for i in range(split):
            m = lax.rem(home + s, groups) * split + i

            @pl.when(m != chip)
            def _():
                ag_got(2 * m + core).wait_recv()
                ag_fwd(m).start()

    def multiply(s):
        cg = lax.rem(home + s, groups)
        for i in range(split):
            ag_got(2 * (cg * split + i) + 1 - core).wait_recv()
        at = pl.ds(pl.multiple_of(cg * GROUP, GROUP), GROUP)
        lanes = []
        for h in range(2):
            first = (2 * cg + h) * split
            part = [ag[first + i] for i in range(split)]
            lanes.append(part[0] if split == 1 else jnp.concatenate(part, axis=0)[0:vecs])
        sc = scale[:, at]
        w = jnp.concatenate(lanes, axis=1) * (sc * sc * factor)
        wh, wl = high(w).astype(F32), rest(w).astype(F32)
        wm = (wh + wl) * mean[:, at]
        member = lax.broadcasted_iota(jnp.int32, (BINS, GROUP), 0) == bins[:, at]
        for r in range(vecs):
            row = slice(r * BINS, (r + 1) * BINS)
            wsp[row, :] = high(jnp.where(member, wh[r:r + 1], 0.0))
            wsp[depth + r * BINS:depth + (r + 1) * BINS, :] = high(jnp.where(member, wl[r:r + 1], 0.0))
            o = jnp.where(member, wm[r:r + 1], 0.0)
            offs[row, :] += o[:, :LANES] + o[:, LANES:]
        for nb in range(samples // GROUP):
            span = slice(nb * GROUP, (nb + 1) * GROUP)
            res = dot_nt(wsp[...], gb[span, at])
            prods[:, span] += res[:depth] + res[depth:]

    if split > 1:
        receive(0)

    @pl.loop(1, groups)
    def _(s):
        receive(s)
        multiply(s - 1)

    multiply(groups - 1)
    off = jnp.sum(offs[...], axis=1, keepdims=True)
    half = (probes // 2) * BINS
    cuts = [(0, half), (half, 2 * half), (2 * half, depth)]
    accs = [jnp.zeros((b - a, b - a), F32) for a, b in cuts]

    for nb in range(samples // GROUP):
        span = slice(nb * GROUP, (nb + 1) * GROUP)
        res = prods[:, span] - off
        prods[:, span] = res
        hi, lo = high(res), rest(res)
        for i, (a, b) in enumerate(cuts):
            h, l = hi[a:b], lo[a:b]
            accs[i] = accs[i] + dot_nt(h, h) + dot_nt(h, l) + dot_nt(l, h)

    strips = []
    for acc in accs:
        size = acc.shape[0]
        same = (lax.broadcasted_iota(jnp.int32, (size, size), 0) // BINS
                == lax.broadcasted_iota(jnp.int32, (size, size), 1) // BINS)
        strips.append(jnp.sum(jnp.where(same, acc, 0.0).reshape(size // BINS, BINS, size), axis=0))
    strips.append(jnp.zeros((BINS, LANES - BINS), F32))
    flat = jnp.concatenate(strips, axis=1)
    width = flat.shape[1] // LANES
    for k in range(BINS):
        for t in range(width):
            p = k * width + t
            gsend[p // per, p % per:p % per + 1, :] = flat[k:k + 1, t * LANES:(t + 1) * LANES]
    for p in range(BINS * width, n * per):
        gsend[p // per, p % per:p % per + 1, :] = jnp.zeros((1, LANES), F32)

    def gr(d, slot):
        return pltpu.make_async_remote_copy(
            gsend.at[d], grecv.at[slot], gr_s.at[d], gr_r.at[slot],
            device_id={"samp": d}, device_id_type=MESH)

    def ga(d, slot):
        return pltpu.make_async_remote_copy(
            gsum.at[slot], gsum.at[slot], ga_s.at[d], ga_r.at[slot],
            device_id={"samp": d}, device_id_type=MESH)

    def peers(body):
        @pl.loop(1, n)
        def _(s):
            body(lax.rem(me + s, n))

    peers(lambda d: gr(d, me).start())
    grecv[me] = gsend[me]
    peers(lambda d: gr(d, d).wait_recv())
    gsum[me] = jnp.sum(grecv[...], axis=0) * (1.0 / total)
    peers(lambda d: ga(d, me).start())
    peers(lambda d: ga(d, d).wait_recv())
    gram[...] = gsum[...]

    def finish(d):
        gr(d, me).wait_send()
        ga(d, me).wait_send()

    peers(finish)

    def finish_chip(m):
        to_owner(m).wait_send()
        ag_chip(m).wait_send()

    others(finish_chip)

    @pl.loop(0, chips)
    def _(m):
        to_sib(m).wait_send()
        ag_fwd(m).wait_send()


def finisher(n, per, width, vecs, prods, gsum, out_hbm, gram, sem):
    third = prods.shape[0] // 3

    def out_copy(i):
        return pltpu.make_async_copy(
            prods.at[i * third:(i + 1) * third], out_hbm.at[i * third:(i + 1) * third],
            sem.at[i])

    for i in range(3):
        out_copy(i).start()
    if n == BINS:
        flat = jnp.concatenate([gsum[:, t, :] for t in range(width)], axis=1)
    else:
        flat = jnp.concatenate(
            [jnp.concatenate([gsum[p // per, p % per:p % per + 1, :]
                              for p in range(k * width, (k + 1) * width)], axis=1)
             for k in range(BINS)], axis=0)
    lanes = width * LANES
    col = lax.broadcasted_iota(jnp.int32, (BINS, lanes), 1)
    mine = (col % BINS) == lax.broadcasted_iota(jnp.int32, (BINS, lanes), 0)
    spread = jnp.concatenate([jnp.where(mine, flat[k:k + 1], 0.0) for k in range(BINS)], axis=0)
    pick = high((lax.broadcasted_iota(jnp.int32, (lanes, LANES), 0) // BINS
                 == lax.broadcasted_iota(jnp.int32, (lanes, LANES), 1)).astype(F32))
    a = high(spread)
    left = spread - a.astype(F32)
    b = high(left)
    c = high(left - b.astype(F32))
    res = dot(a, pick) + dot(b, pick) + dot(c, pick)
    gram[...] = res[:, :vecs].reshape(BINS, BINS, vecs)
    for i in range(3):
        out_copy(i).wait()


def shards(genotypes, probe_signs, phenotype, marker_mean, marker_scale, marker_bin):
    samples, markers = genotypes.shape
    probes = probe_signs.shape[0]
    vecs = probes + 1
    n = lax.axis_size("samp")
    total = float(samples * n)
    chunks = markers // LANES
    split = n // chunks
    rows = -(-vecs // split)
    width = -(-(vecs * BINS) // LANES)
    per = -(-(BINS * width) // n)
    chips = n // 2
    groups = markers // GROUP
    vm = pltpu.VMEM
    dma = pltpu.SemaphoreType.DMA
    vspec = pl.BlockSpec(memory_space=pltpu.VMEM)
    hbmspec = pl.BlockSpec(memory_space=pltpu.HBM)
    anyspec = pl.BlockSpec(memory_space=pl.ANY)
    products, gram = pl.pallas_call(
        functools.partial(kernel, n, split, rows, per, total),
        out_shape=(vm((vecs * BINS, samples), F32), vm((n, per, LANES), F32)),
        in_specs=[hbmspec] * 6,
        out_specs=(vspec, vspec),
        scratch_shapes=[
            vm(probe_signs.shape, jnp.int32),
            vm((1, samples), F32),
            vm((1, markers), F32),
            vm((1, markers), F32),
            vm((1, markers), jnp.int32),
            vm((groups, samples, GROUP), jnp.int32),
            vm((samples, markers), BF),
            vm((probes + 16, samples), BF),
            vm((chips, 2, rows, LANES), F32),
            vm((chips, rows, LANES), F32),
            vm((chips, rows, LANES), F32),
            vm((chips, rows, LANES), F32),
            vm((n, rows, LANES), F32),
            vm((2 * vecs * BINS, GROUP), BF),
            vm((vecs * BINS, LANES), F32),
            vm((n, per, LANES), F32),
            vm((n, per, LANES), F32),
            vm((n, per, LANES), F32),
            dma((5,)), dma((groups,)),
            dma((chips,)), dma((chips,)), dma((chips,)), dma((chips,)),
            dma((chips,)), dma((n,)), dma((chips,)),
            dma((n,)), dma((n,)), dma((n,)), dma((n,)),
        ],
        compiler_params=pltpu.CompilerParams(
            collective_id=0, has_side_effects=True, vmem_limit_bytes=32 * 1024 * 1024),
    )(*[pltpu.with_memory_space_constraint(x, pltpu.HBM) for x in (
        genotypes, probe_signs, phenotype[None, :], marker_mean[None, :],
        marker_scale[None, :], marker_bin[None, :])])
    products, gram = pl.pallas_call(
        functools.partial(finisher, n, per, width, vecs),
        out_shape=(jax.ShapeDtypeStruct((vecs * BINS, samples), F32),
                   jax.ShapeDtypeStruct((BINS, BINS, vecs), F32)),
        in_specs=[vspec, vspec],
        out_specs=(anyspec, vspec),
        scratch_shapes=[dma((3,))],
        compiler_params=pltpu.CompilerParams(vmem_limit_bytes=16 * 1024 * 1024),
    )(products, gram)
    return products.reshape(vecs, BINS, samples).transpose(1, 0, 2), gram


def solution(mesh):
    in_specs = (
        P(("grp", "samp"), None),
        P(None, ("grp", "samp")),
        P(("grp", "samp")),
        P(),
        P(),
        P(),
    )
    out_specs = (P(None, None, ("grp", "samp")), P("grp", None, None))
    return jax.shard_map(shards, mesh=mesh, in_specs=in_specs, out_specs=out_specs, check_vma=False)
```

```python
import functools
import math

import jax
import jax.numpy as jnp
from jax import lax
from jax.experimental import pallas as pl
from jax.experimental.pallas import tpu as pltpu
from jax.sharding import PartitionSpec as P

BINS = 16
M_BIN = 128
LANES = 128
GROUP = 256
BF = jnp.bfloat16
F32 = jnp.float32
MESH = pl.DeviceIdType.MESH
NT = (((1,), (1,)), ((), ()))


def dot(a, b):
    return jnp.dot(a, b, preferred_element_type=F32)


def dot_nt(a, b):
    return lax.dot_general(a, b, NT, preferred_element_type=F32)


def high(x):
    return x.astype(BF)


def rest(x):
    return (x - x.astype(BF).astype(F32)).astype(BF)


def kernel(n, split, rows, per, total, g_hbm, probe_hbm, pheno_hbm, mean_hbm, scale_hbm, bins_hbm, prods, gram,
           probe, pheno, mean, scale, bins,
           gbuf, gb, vec, tsend, sibrecv, rsend, rsrecv, ag, wsp, offs, gsend, grecv, gsum,
           small_sem, in_sem, sib_s, sib_r, rs_s, rs_r, ag_s, ag_r, fwd_s, gr_s, gr_r, ga_s, ga_r):
    me = lax.axis_index("samp")
    chip, core = me // 2, me % 2
    chips = n // 2
    sib = me + 1 - 2 * core
    samples, markers = g_hbm.shape
    probes = probe.shape[0]
    vecs = probes + 1
    groups = markers // GROUP
    home = chip // split

    barrier = pltpu.get_barrier_semaphore()

    @pl.loop(1, n)
    def _(s):
        pl.semaphore_signal(barrier, inc=1, device_id={"samp": lax.rem(me + s, n)}, device_id_type=MESH)

    def near(s):
        if groups & (groups - 1):
            return lax.rem(home + s, groups)
        return sum(2 ** b * ((home // 2 ** b + s // 2 ** b) % 2)
                   for b in range(groups.bit_length() - 1))

    def cg_of(q):
        return near(groups - 1 - q)

    def cols(q):
        return pl.ds(pl.multiple_of(cg_of(q) * GROUP, GROUP), GROUP)

    def load(q):
        return pltpu.make_async_copy(g_hbm.at[:, cols(q)], gbuf.at[q], in_sem.at[q])

    small = [pltpu.make_async_copy(src, dst, small_sem.at[i]) for i, (src, dst) in enumerate(
        [(probe_hbm, probe), (pheno_hbm, pheno), (mean_hbm, mean), (scale_hbm, scale), (bins_hbm, bins)])]
    for copy in small:
        copy.start()
    for q in range(groups):
        load(q).start()

    def to_sib(m):
        return pltpu.make_async_remote_copy(
            tsend.at[m, 1 - core], sibrecv.at[m], sib_s.at[m], sib_r.at[m],
            device_id={"samp": sib}, device_id_type=MESH)

    def to_owner(m):
        return pltpu.make_async_remote_copy(
            rsend.at[m], rsrecv.at[chip], rs_s.at[m], rs_r.at[chip],
            device_id={"samp": 2 * m + core}, device_id_type=MESH)

    def from_owner(m):
        return pltpu.make_async_remote_copy(
            rsend.at[m], rsrecv.at[m], rs_s.at[m], rs_r.at[m],
            device_id={"samp": 2 * m + core}, device_id_type=MESH)

    for copy in small:
        copy.wait()
    signs = (2 * probe[...] - 1).astype(F32)
    ph = pheno[...]
    ph_mid = ph - high(ph).astype(F32)
    vec[0:probes, :] = high(signs)
    tail = jnp.concatenate(
        [ph, ph_mid, ph_mid - high(ph_mid).astype(F32), jnp.zeros((13, samples), F32)], axis=0)
    vec[probes:probes + 16, :] = high(tail)
    sum_p = jnp.sum(signs, axis=1, keepdims=True)
    sum_y = jnp.sum(ph, axis=1, keepdims=True)

    def combine(q):
        for i in range(split):
            m = cg_of(q) * split + i
            to_sib(m).wait_recv()
            both = tsend[m, core] + sibrecv[m]
            if split == 1:
                if q == groups - 1:
                    rsrecv[m] = both
                else:
                    rsend[m] = both
                    to_owner(m).start()
            else:
                @pl.when(m == chip)
                def _():
                    rsrecv[m] = both

                @pl.when(m != chip)
                def _():
                    rsend[m] = both
                    to_owner(m).start()

    for q in range(groups):
        load(q).wait()
        part = gbuf[q].astype(F32).astype(BF)
        gb[:, cols(q)] = part
        t = dot(vec[...], part)
        mu = mean[:, cols(q)]
        tp = t[0:probes] - sum_p * mu
        ty = t[probes:probes + 1] + t[probes + 1:probes + 2] + t[probes + 2:probes + 3] - sum_y * mu
        cg = cg_of(q)
        if split == 1:
            for h in range(2):
                at = slice(h * LANES, (h + 1) * LANES)
                tsend[cg, h, 0:probes, :] = tp[:, at]
                tsend[cg, h, probes:vecs, :] = ty[:, at]
        else:
            whole = jnp.concatenate([tp, ty, jnp.zeros((split * rows - vecs, GROUP), F32)], axis=0)
            for h in range(2):
                for s in range(split):
                    tsend[cg * split + (h * split + s) // 2, s % 2] = whole[
                        s * rows:(s + 1) * rows, h * LANES:(h + 1) * LANES]
        if q == 0:
            pl.semaphore_wait(barrier, n - 1)
        for i in range(split):
            to_sib(cg * split + i).start()
        if q > 0:
            combine(q - 1)
    combine(groups - 1)

    def others(body):
        @pl.loop(1, chips)
        def _(s):
            body(lax.rem(chip + s, chips))

    others(lambda m: from_owner(m).wait_recv())
    ag[me] = jnp.sum(rsrecv[...], axis=0)

    def ag_chip(m):
        return pltpu.make_async_remote_copy(
            ag.at[me], ag.at[me], ag_s.at[m], ag_r.at[me],
            device_id={"samp": 2 * m + core}, device_id_type=MESH)

    def ag_fwd(m):
        return pltpu.make_async_remote_copy(
            ag.at[2 * m + core], ag.at[2 * m + core], fwd_s.at[m], ag_r.at[2 * m + core],
            device_id={"samp": sib}, device_id_type=MESH)

    def ag_got(d):
        return pltpu.make_async_remote_copy(
            ag.at[d], ag.at[d], fwd_s.at[chip], ag_r.at[d],
            device_id={"samp": sib}, device_id_type=MESH)

    if split == 1:
        @pl.loop(1, groups)
        def _(s):
            ag_chip(near(s)).start()
    else:
        others(lambda m: ag_chip(m).start())
    ag_fwd(chip).start()

    factor = 1.0 / (math.sqrt(total) * math.sqrt(M_BIN))
    depth = vecs * BINS
    prods[...] = jnp.zeros_like(prods)
    offs[...] = jnp.zeros_like(offs)

    def receive(s):
        for i in range(split):
            m = near(s) * split + i

            @pl.when(m != chip)
            def _():
                ag_got(2 * m + core).wait_recv()
                ag_fwd(m).start()

    def multiply(s):
        cg = near(s)
        for i in range(split):
            ag_got(2 * (cg * split + i) + 1 - core).wait_recv()
        at = pl.ds(pl.multiple_of(cg * GROUP, GROUP), GROUP)
        lanes = []
        for h in range(2):
            first = (2 * cg + h) * split
            part = [ag[first + i] for i in range(split)]
            lanes.append(part[0] if split == 1 else jnp.concatenate(part, axis=0)[0:vecs])
        sc = scale[:, at]
        w = jnp.concatenate(lanes, axis=1) * (sc * sc * factor)
        wh, wl = high(w).astype(F32), rest(w).astype(F32)
        wm = (wh + wl) * mean[:, at]
        member = lax.broadcasted_iota(jnp.int32, (BINS, GROUP), 0) == bins[:, at]
        for r in range(vecs):
            row = slice(r * BINS, (r + 1) * BINS)
            wsp[row, :] = high(jnp.where(member, wh[r:r + 1], 0.0))
            wsp[depth + r * BINS:depth + (r + 1) * BINS, :] = high(jnp.where(member, wl[r:r + 1], 0.0))
            o = jnp.where(member, wm[r:r + 1], 0.0)
            offs[row, :] += o[:, :LANES] + o[:, LANES:]
        for nb in range(samples // GROUP):
            span = slice(nb * GROUP, (nb + 1) * GROUP)
            res = dot_nt(wsp[...], gb[span, at])
            prods[:, span] += res[:depth] + res[depth:]

    if split > 1:
        receive(0)

    @pl.loop(1, groups)
    def _(s):
        receive(s)
        multiply(s - 1)

    multiply(groups - 1)
    off = jnp.sum(offs[...], axis=1, keepdims=True)
    half = (probes // 2) * BINS
    cuts = [(0, half), (half, 2 * half), (2 * half, depth)]
    accs = [jnp.zeros((b - a, b - a), F32) for a, b in cuts]

    for nb in range(samples // GROUP):
        span = slice(nb * GROUP, (nb + 1) * GROUP)
        res = prods[:, span] - off
        prods[:, span] = res
        hi, lo = high(res), rest(res)
        for i, (a, b) in enumerate(cuts):
            h, l = hi[a:b], lo[a:b]
            accs[i] = accs[i] + dot_nt(h, h) + dot_nt(h, l) + dot_nt(l, h)

    strips = []
    for acc in accs:
        size = acc.shape[0]
        same = (lax.broadcasted_iota(jnp.int32, (size, size), 0) // BINS
                == lax.broadcasted_iota(jnp.int32, (size, size), 1) // BINS)
        strips.append(jnp.sum(jnp.where(same, acc, 0.0).reshape(size // BINS, BINS, size), axis=0))
    strips.append(jnp.zeros((BINS, LANES - BINS), F32))
    flat = jnp.concatenate(strips, axis=1)
    width = flat.shape[1] // LANES
    for k in range(BINS):
        for t in range(width):
            p = k * width + t
            gsend[p // per, p % per:p % per + 1, :] = flat[k:k + 1, t * LANES:(t + 1) * LANES]
    for p in range(BINS * width, n * per):
        gsend[p // per, p % per:p % per + 1, :] = jnp.zeros((1, LANES), F32)

    def gr(d, slot):
        return pltpu.make_async_remote_copy(
            gsend.at[d], grecv.at[slot], gr_s.at[d], gr_r.at[slot],
            device_id={"samp": d}, device_id_type=MESH)

    def ga(d, slot):
        return pltpu.make_async_remote_copy(
            gsum.at[slot], gsum.at[slot], ga_s.at[d], ga_r.at[slot],
            device_id={"samp": d}, device_id_type=MESH)

    def peers(body):
        @pl.loop(1, n)
        def _(s):
            body(lax.rem(me + s, n))

    peers(lambda d: gr(d, me).start())
    grecv[me] = gsend[me]
    peers(lambda d: gr(d, d).wait_recv())
    gsum[me] = jnp.sum(grecv[...], axis=0) * (1.0 / total)
    peers(lambda d: ga(d, me).start())
    peers(lambda d: ga(d, d).wait_recv())
    gram[...] = gsum[...]

    def finish(d):
        gr(d, me).wait_send()
        ga(d, me).wait_send()

    peers(finish)

    def finish_chip(m):
        to_owner(m).wait_send()
        ag_chip(m).wait_send()

    others(finish_chip)

    @pl.loop(0, chips)
    def _(m):
        to_sib(m).wait_send()
        ag_fwd(m).wait_send()


def finisher(n, per, width, vecs, prods, gsum, out_hbm, gram, sem):
    third = prods.shape[0] // 3

    def out_copy(i):
        return pltpu.make_async_copy(
            prods.at[i * third:(i + 1) * third], out_hbm.at[i * third:(i + 1) * third],
            sem.at[i])

    for i in range(3):
        out_copy(i).start()
    if n == BINS:
        flat = jnp.concatenate([gsum[:, t, :] for t in range(width)], axis=1)
    else:
        flat = jnp.concatenate(
            [jnp.concatenate([gsum[p // per, p % per:p % per + 1, :]
                              for p in range(k * width, (k + 1) * width)], axis=1)
             for k in range(BINS)], axis=0)
    lanes = width * LANES
    col = lax.broadcasted_iota(jnp.int32, (BINS, lanes), 1)
    mine = (col % BINS) == lax.broadcasted_iota(jnp.int32, (BINS, lanes), 0)
    spread = jnp.concatenate([jnp.where(mine, flat[k:k + 1], 0.0) for k in range(BINS)], axis=0)
    pick = high((lax.broadcasted_iota(jnp.int32, (lanes, LANES), 0) // BINS
                 == lax.broadcasted_iota(jnp.int32, (lanes, LANES), 1)).astype(F32))
    a = high(spread)
    left = spread - a.astype(F32)
    b = high(left)
    c = high(left - b.astype(F32))
    res = dot(a, pick) + dot(b, pick) + dot(c, pick)
    gram[...] = res[:, :vecs].reshape(BINS, BINS, vecs)
    for i in range(3):
        out_copy(i).wait()


def shards(genotypes, probe_signs, phenotype, marker_mean, marker_scale, marker_bin):
    samples, markers = genotypes.shape
    probes = probe_signs.shape[0]
    vecs = probes + 1
    n = lax.axis_size("samp")
    total = float(samples * n)
    chunks = markers // LANES
    split = n // chunks
    rows = -(-vecs // split)
    width = -(-(vecs * BINS) // LANES)
    per = -(-(BINS * width) // n)
    chips = n // 2
    groups = markers // GROUP
    vm = pltpu.VMEM
    dma = pltpu.SemaphoreType.DMA
    vspec = pl.BlockSpec(memory_space=pltpu.VMEM)
    hbmspec = pl.BlockSpec(memory_space=pltpu.HBM)
    anyspec = pl.BlockSpec(memory_space=pl.ANY)
    products, gram = pl.pallas_call(
        functools.partial(kernel, n, split, rows, per, total),
        out_shape=(vm((vecs * BINS, samples), F32), vm((n, per, LANES), F32)),
        in_specs=[hbmspec] * 6,
        out_specs=(vspec, vspec),
        scratch_shapes=[
            vm(probe_signs.shape, jnp.int32),
            vm((1, samples), F32),
            vm((1, markers), F32),
            vm((1, markers), F32),
            vm((1, markers), jnp.int32),
            vm((groups, samples, GROUP), jnp.int32),
            vm((samples, markers), BF),
            vm((probes + 16, samples), BF),
            vm((chips, 2, rows, LANES), F32),
            vm((chips, rows, LANES), F32),
            vm((chips, rows, LANES), F32),
            vm((chips, rows, LANES), F32),
            vm((n, rows, LANES), F32),
            vm((2 * vecs * BINS, GROUP), BF),
            vm((vecs * BINS, LANES), F32),
            vm((n, per, LANES), F32),
            vm((n, per, LANES), F32),
            vm((n, per, LANES), F32),
            dma((5,)), dma((groups,)),
            dma((chips,)), dma((chips,)), dma((chips,)), dma((chips,)),
            dma((chips,)), dma((n,)), dma((chips,)),
            dma((n,)), dma((n,)), dma((n,)), dma((n,)),
        ],
        compiler_params=pltpu.CompilerParams(
            collective_id=0, has_side_effects=True, vmem_limit_bytes=32 * 1024 * 1024),
    )(*[pltpu.with_memory_space_constraint(x, pltpu.HBM) for x in (
        genotypes, probe_signs, phenotype[None, :], marker_mean[None, :],
        marker_scale[None, :], marker_bin[None, :])])
    products, gram = pl.pallas_call(
        functools.partial(finisher, n, per, width, vecs),
        out_shape=(jax.ShapeDtypeStruct((vecs * BINS, samples), F32),
                   jax.ShapeDtypeStruct((BINS, BINS, vecs), F32)),
        in_specs=[vspec, vspec],
        out_specs=(anyspec, vspec),
        scratch_shapes=[dma((3,))],
        compiler_params=pltpu.CompilerParams(vmem_limit_bytes=16 * 1024 * 1024),
    )(products, gram)
    return products.reshape(vecs, BINS, samples).transpose(1, 0, 2), gram


def solution(mesh):
    in_specs = (
        P(("grp", "samp"), None),
        P(None, ("grp", "samp")),
        P(("grp", "samp")),
        P(),
        P(),
        P(),
    )
    out_specs = (P(None, None, ("grp", "samp")), P("grp", None, None))
    return jax.shard_map(shards, mesh=mesh, in_specs=in_specs, out_specs=out_specs, check_vma=False)
```
